256 devices in a mesh: cell: 16 (over y_hi, z), region: 16 (over x, y_lo, core).
Axes of the slice: x: 4, y: 4 (y_hi: 2, y_lo: 2; y = y_hi * 2 + y_lo), z: 8, core: 2. Of those that a mesh axis runs over, the one named last changes fastest.
Arguments:
- observed: bfloat16 [16384, 65536], P('cell', 'region'), may hold values from -0.5 to 0.5
- block_mask: int32 [2048, 512], P('cell', 'region'), may hold values 0 or 1
- plan: int32 [4], replicated, may hold values from 0 to 3, each once
- cell_factors: float32 [16384, 256], P('cell'), may hold values from -6 to 6
- region_factors: float32 [262144, 256], P(('cell', 'region')), may hold values from -6 to 6
Outputs:
- new_cells: float32 [16384, 256], P('cell')
- new_regions: float32 [262144, 256], P(('cell', 'region'))
The draws below stay inside these ranges and needn't reach their ends.
Inputs may be any that keep to these rules, and one draw needn't show every extreme that they name: `plan`: each stored slot 0 to 3 appears once.
All inputs are finite; a program needn't handle non-finite values. No bound on the sum of `block_mask` on one device may be relied on, other than what follows from the above.
Results may differ from the reference program's by a relative error of at most 0.0056.
Values sent between devices are 32-bit elements; how exact they have to be, the bound alone decides.
A program may use at most 64 MiB of HBM per device.

```python
import math
import jax
import jax.numpy as jnp
from jax import lax

K = 256
CELL_DEV = 1024
SUB = 1024
STRATA = 4
CELLS = 16384
REGION_BLOCKS = 256
WINDOW_COLS = 65536
N_CELL = 16
N_REGION = 16


def plant(array, stream_key, least, top_value):
    longest = array.shape.index(max(array.shape))
    spots = []
    for shift in (0, 1):
        where = [jax.random.randint(jax.random.fold_in(stream_key, axis), (), 0, length) for axis, length in enumerate(array.shape)]
        where[longest] = (where[longest] + shift) % array.shape[longest]
        spots.append(tuple(where))
    return array.at[spots[0]].set(least).at[spots[1]].set(top_value)


def levels(stream_key, shape, cuts, low, high):
    def one(axis_at, parts):
        heights = jax.random.uniform(jax.random.fold_in(jax.random.fold_in(stream_key, 6), axis_at), (parts,), jnp.float32, low / len(cuts), high / len(cuts))
        return jnp.repeat(jnp.exp(heights), shape[axis_at] // parts).reshape((-1,) + (1,) * (len(shape) - axis_at - 1))

    level = one(*cuts[0])
    for cut in cuts[1:]:
        level = level * one(*cut)
    return level


def scatter_about(stream_key, dims, width, reach, cuts=(), held_as=jnp.bfloat16):
    array = jax.random.normal(stream_key, dims, jnp.float32) * width
    if len(cuts) > 0:
        array = levels(stream_key, dims, cuts, -0.22, 0.18) * array
    return jnp.clip(array, min=-reach, max=reach).astype(held_as)


def setup_inputs(seed: int = 0) -> dict:
    key_of = jax.random.split(jax.random.key(seed), 6)
    return {
        "observed": jnp.clip(jax.random.uniform(key_of[0], (CELLS, WINDOW_COLS), jnp.float32, -0.5, 0.5) * levels(key_of[0], (CELLS, WINDOW_COLS), ((0, 16), (1, 16)), -0.4, 0.0), -0.5, 0.5).astype(jnp.bfloat16),
        "block_mask": plant((jax.random.randint(key_of[1], (CELLS // 8, WINDOW_COLS // 128), 0, 5) < 3).astype(jnp.int32), jax.random.fold_in(key_of[1], 1), 0, 1),
        "plan": jax.random.permutation(key_of[2], STRATA).astype(jnp.int32),
        "cell_factors": scatter_about(key_of[3], (CELLS, K), 1.0, 6.0, ((0, 16),), jnp.float32),
        "region_factors": scatter_about(key_of[4], (REGION_BLOCKS * SUB, K), 1.0, 6.0, ((0, 256),), jnp.float32),
    }


beta_mom = 0.9

def reference(observed, block_mask, plan, cell_factors, region_factors):
    total_cols = N_REGION * SUB
    scale_pred = 0.5 / math.sqrt(total_cols)
    rate_region = total_cols / CELL_DEV
    data_tiles = observed.reshape(N_CELL, CELL_DEV, N_REGION, STRATA, SUB)
    mask_tiles = block_mask.reshape(N_CELL, CELL_DEV // 8, N_REGION, STRATA, SUB // 128)
    cells_now = cell_factors.reshape(N_CELL, CELL_DEV, K)
    regions_now = region_factors.reshape(N_CELL, N_REGION, SUB, K)
    momentum = jnp.zeros_like(cells_now)

    def block_grads(items):
        cell_rows, data_block, mask_block, region_block = items
        cell_bf = cell_rows.astype(jnp.bfloat16).astype(jnp.float32)
        region_bf = region_block.astype(jnp.bfloat16).astype(jnp.float32)
        predicted = jnp.einsum('rk,jck->rjc', cell_bf, region_bf)
        expanded = jnp.broadcast_to(mask_block[:, None, :, :, None], (CELL_DEV // 8, 8, N_REGION, SUB // 128, 128))
        expanded = expanded.reshape(CELL_DEV, N_REGION, SUB).astype(jnp.float32)
        resid = (expanded * (scale_pred * predicted - data_block.astype(jnp.float32))).astype(jnp.bfloat16)
        resid_f = resid.astype(jnp.float32)
        grad_cell = scale_pred * jnp.einsum('rjc,jck->rk', resid_f, region_bf)
        grad_region = scale_pred * jnp.einsum('rjc,rk->jck', resid_f, cell_bf)
        return (grad_cell, grad_region)
    for section in range(STRATA):
        slot_index = plan[section]
        data_slot = lax.dynamic_index_in_dim(data_tiles, slot_index, 3, keepdims=False)
        mask_slot = lax.dynamic_index_in_dim(mask_tiles, slot_index, 3, keepdims=False)
        chosen = jnp.roll(regions_now, -section, axis=0)
        grad_cells, grad_regions = lax.map(block_grads, (cells_now, data_slot, mask_slot, chosen))
        regions_now = regions_now - rate_region * jnp.roll(grad_regions, section, axis=0)
        momentum = beta_mom * momentum + grad_cells
        cells_now = cells_now - momentum
    return (cells_now.reshape(CELLS, K), regions_now.reshape(REGION_BLOCKS * SUB, K))
```

```python
import functools
import math

import jax
import jax.numpy as jnp
from jax import lax
from jax.experimental import pallas as pl
from jax.experimental.pallas import tpu as pltpu
from jax.sharding import PartitionSpec as P

STRATA = 4
MOMENTUM = 0.9
ROWS = 1024
RANK = 256
CHUNK = 256
CHUNKS = ROWS // CHUNK
HALF = ROWS // 2
PIECE = 64
RET = 128
RETS = ROWS // RET
DOWN = (0, 2, 4)
RAW, FINAL, TURN, RELAY = 4, 7, 8, 9
NT = (((1,), (1,)), ((), ()))
TN = (((0,), (0,)), ((), ()))


def remote(src, dst, send, recv, cell, region):
    return pltpu.make_async_remote_copy(
        src_ref=src,
        dst_ref=dst,
        send_sem=send,
        recv_sem=recv,
        device_id={"cell": cell, "region": region},
        device_id_type=pl.DeviceIdType.MESH,
    )


def kernel(
    scale, rate, plan, mask, y_hbm, u_hbm, v_hbm, out_u, out_v,
    ybuf, vbuf, ubuf, gbuf, core_buf, sum_buf, expanded, resid, u_bf, u_scaled, moment,
    load_sem, shift_send, shift_recv, pass_send,
    core_send, core_recv, rs_send, rs_recv, ag_send, ag_recv, agc_send, agc_recv,
    ret_send, ret_recv, relay_send, relay_recv, turn_send, turn_recv, out_sem,
):
    cell, region = lax.axis_index("cell"), lax.axis_index("region")
    z, core, chip = cell % 8, region % 2, region // 2
    ring = cell - z
    across = (cell + 8) % 16
    other_core = region + 1 - 2 * core

    def along(steps):
        return ring + (z + steps + 8) % 8

    def peer(d):
        return ((chip + d) % 8) * 2 + core

    def v_rows(slot, k):
        return vbuf.at[slot, pl.ds(k * CHUNK, CHUNK)]

    def ret_rows(slot, p):
        return vbuf.at[slot, pl.ds(p * RET, RET)]

    loads = [
        pltpu.make_async_copy(u_hbm, ubuf.at[0], load_sem.at[0]),
        pltpu.make_async_copy(v_hbm, vbuf.at[0], load_sem.at[1]),
    ] + [
        pltpu.make_async_copy(y_hbm.at[:, pl.ds(q * ROWS, ROWS)], ybuf.at[q], load_sem.at[2 + q]) for q in range(STRATA)
    ]
    for load in loads:
        load.start()

    barrier = pltpu.get_barrier_semaphore()
    greeted = [(cell, other_core)] + [(cell, peer(d)) for d in range(1, 8)]
    greeted += [(along(d), region) for d in (-1, 1, -3, 3, -2, 2)] + [(across, region)]
    for c, r in greeted:
        pl.semaphore_signal(
            barrier, inc=1, device_id={"cell": c, "region": r}, device_id_type=pl.DeviceIdType.MESH
        )
    moment[...] = jnp.zeros_like(moment)
    mask_bf = mask[...].astype(jnp.float32).astype(jnp.bfloat16)
    block = lax.broadcasted_iota(jnp.int32, (32, ROWS), 0)
    lane = lax.broadcasted_iota(jnp.int32, (32, ROWS), 1)
    for q in range(STRATA):
        chosen = (block == q * 8 + lane // 128).astype(jnp.float32).astype(jnp.bfloat16)
        expanded[q] = jnp.dot(mask_bf, chosen, preferred_element_type=jnp.float32)
    for load in loads:
        load.wait()
    pl.semaphore_wait(barrier, len(greeted))

    is0 = 1 - (z + 7) // 8
    mine = core * HALF + chip * PIECE

    def shift_copy(s, k):
        slot = s + 1 + is0 * (RAW - 1)
        first = along(-1)
        to = first if k < 2 else first + is0 * (across - first)
        return remote(v_rows(s, k), v_rows(slot, k), shift_send.at[s, k], shift_recv.at[slot, k], to, region)

    def shift_copy_in(s, k):
        remote(v_rows(s, k), v_rows(s, k), shift_send.at[0, k], shift_recv.at[s, k], cell, region).wait_recv()

    def pass_on(s, k, to):
        remote(v_rows(RAW + s, k), v_rows(RAW + s, k), pass_send.at[s, k], shift_recv.at[RAW + s, k], to, region).wait_recv()
        remote(v_rows(RAW + s, k), v_rows(s + 1, k), pass_send.at[s, k], shift_recv.at[s + 1, k], to, region).start()

    def pass_wait(s, k, to):
        remote(v_rows(RAW + s, k), v_rows(s + 1, k), pass_send.at[s, k], shift_recv.at[s + 1, k], to, region).wait_send()

    def ret_copy(p):
        slot = FINAL + (z + 3) // 8
        return remote(ret_rows(3, p), ret_rows(slot, p), ret_send.at[p], ret_recv.at[slot - FINAL, p], along(3), region)

    def ret_copy_down(p):
        return remote(ret_rows(3, p), ret_rows(RELAY, p), ret_send.at[p], relay_recv.at[p], along(-3), region)

    def relay_copy(p):
        source = (z + 3) % 8
        slot = FINAL + (source + 3) // 8
        return remote(ret_rows(RELAY, p), ret_rows(slot, p), relay_send.at[p], ret_recv.at[slot - FINAL, p], along(-2), region)

    def turn_copy(p):
        return remote(ret_rows(TURN, p), ret_rows(FINAL, p), turn_send.at[p], ret_recv.at[0, p], across, region)

    def core_copy(s):
        away = pl.ds((1 - core) * HALF, HALF)
        return remote(gbuf.at[s, away], core_buf.at[s], core_send.at[s], core_recv.at[s], cell, other_core)

    def rs_copy(s, d):
        rows = pl.ds(core * HALF + ((chip + d) % 8) * PIECE, PIECE)
        return remote(gbuf.at[s, rows], sum_buf.at[s, d], rs_send.at[s, d], rs_recv.at[s, d], cell, peer(d))

    def ag_copy(s, d):
        rows = pl.ds(mine, PIECE)
        return remote(ubuf.at[s + 1, rows], ubuf.at[s + 1, rows], ag_send.at[s, d], ag_recv.at[s, d], cell, peer(d))

    def agc_copy(s, d):
        rows = pl.ds(core * HALF + ((chip - d + 8) % 8) * PIECE, PIECE)
        return remote(ubuf.at[s + 1, rows], ubuf.at[s + 1, rows], agc_send.at[s, d], agc_recv.at[s, d], cell, other_core)

    def prepare(s):
        u = ubuf[s].astype(jnp.bfloat16)
        u_bf[...] = u
        u_scaled[...] = u * jnp.bfloat16(scale)

    def chunk(s, k):
        v_bf = vbuf[s, pl.ds(k * CHUNK, CHUNK), :].astype(jnp.bfloat16)
        q, columns = plan[s], pl.ds(k * CHUNK, CHUNK)
        for m in range(4):
            base = pl.multiple_of(((1 - core) * HALF + m * 256) % ROWS, 256)
            rows = pl.ds(base, 256)
            predicted = lax.dot_general(u_scaled[rows, :], v_bf, NT, preferred_element_type=jnp.float32)
            w = expanded[q, pl.ds(pl.multiple_of(base // 8, 32), 32), columns]
            w = jnp.broadcast_to(w[:, None, :], (32, 8, CHUNK)).reshape(256, CHUNK)
            r = (w * (predicted - ybuf[q, rows, columns].astype(jnp.float32))).astype(jnp.bfloat16)
            resid[rows, :] = r
            g = scale * jnp.dot(r, v_bf, preferred_element_type=jnp.float32)
            gbuf[s, rows, :] = g if k == 0 else gbuf[s, rows, :] + g
            if k == CHUNKS - 1 and m == 1:
                core_copy(s).start()
        h = scale * lax.dot_general(resid[...], u_bf[...], TN, preferred_element_type=jnp.float32)
        vbuf[s, pl.ds(k * CHUNK, CHUNK), :] = vbuf[s, pl.ds(k * CHUNK, CHUNK), :] - rate * h

    def reduce_core(s):
        core_copy(s).wait_recv()
        own = pl.ds(pl.multiple_of(core * HALF, HALF), HALF)
        gbuf[s, own, :] = gbuf[s, own, :] + core_buf[s]
        for d in (4, 3, 5, 2, 6, 1, 7):
            rs_copy(s, d).start()

    def reduce_chips(s):
        rows = pl.ds(pl.multiple_of(mine, PIECE), PIECE)
        total = gbuf[s, rows, :]
        for d in range(1, 8):
            rs_copy(s, d).wait_recv()
            total = total + sum_buf[s, d]
        step = MOMENTUM * moment[...] + total
        moment[...] = step
        ubuf[s + 1, rows, :] = ubuf[s, rows, :] - step
        for d in (4, 3, 5, 2, 6, 1, 7):
            ag_copy(s, d).start()
        agc_copy(s, 0).start()

    def gather(s):
        for d in range(1, 8):
            ag_copy(s, d).wait_recv()
            agc_copy(s, d).start()
        for d in range(8):
            agc_copy(s, d).wait_recv()

    @pl.loop(0, STRATA - 1)
    def _(s):
        prepare(s)
        for k in range(CHUNKS):
            @pl.when(s > 0)
            def _():
                shift_copy_in(s, k)
            chunk(s, k)
            shift_copy(s, k).start()
        reduce_core(s)

        @pl.when(z == 7)
        def _():
            pass_on(s, 0, across)

        @pl.when(z == 0)
        def _():
            pass_on(s, 2, along(-1))
            pass_on(s, 3, along(-1))

        reduce_chips(s)

        @pl.when(z == 7)
        def _():
            pass_on(s, 1, across)

        gather(s)

    s = STRATA - 1
    prepare(s)
    for k in range(CHUNKS):
        shift_copy_in(s, k)
        chunk(s, k)
        for p in (2 * k, 2 * k + 1):
            (ret_copy_down(p) if p in DOWN else ret_copy(p)).start()
    reduce_core(s)

    def relay(p):
        ret_copy_down(p).wait_recv()
        relay_copy(p).start()

    relay(DOWN[0])
    reduce_chips(s)
    relay(DOWN[1])
    gather(s)
    store_u = pltpu.make_async_copy(ubuf.at[STRATA], out_u, out_sem.at[RETS])
    store_u.start()
    relay(DOWN[2])

    order = (1, 3, 0, 5, 2, 6, 4, 7)

    @pl.when(z < 3)
    def _():
        for p in order:
            remote(ret_rows(TURN, p), ret_rows(TURN, p), ret_send.at[p], ret_recv.at[1, p], cell, region).wait_recv()
            turn_copy(p).start()

    stores = []
    for p in order:
        remote(ret_rows(FINAL, p), ret_rows(FINAL, p), ret_send.at[p], ret_recv.at[0, p], cell, region).wait_recv()
        store = pltpu.make_async_copy(vbuf.at[FINAL, pl.ds(p * RET, RET)], out_v.at[pl.ds(p * RET, RET)], out_sem.at[p])
        store.start()
        stores.append(store)

    @pl.loop(0, STRATA)
    def _(s):
        core_copy(s).wait_send()
        for d in range(1, 8):
            rs_copy(s, d).wait_send()
            ag_copy(s, d).wait_send()
        for d in range(8):
            agc_copy(s, d).wait_send()

    @pl.loop(0, STRATA - 1)
    def _(s):
        for k in range(CHUNKS):
            shift_copy(s, k).wait_send()

        @pl.when(z == 7)
        def _():
            pass_wait(s, 0, across)
            pass_wait(s, 1, across)

        @pl.when(z == 0)
        def _():
            pass_wait(s, 2, along(-1))
            pass_wait(s, 3, along(-1))

    for p in range(RETS):
        (ret_copy_down(p) if p in DOWN else ret_copy(p)).wait_send()
    for p in DOWN:
        relay_copy(p).wait_send()

    @pl.when(z < 3)
    def _():
        for p in order:
            turn_copy(p).wait_send()

    store_u.wait()
    for store in stores:
        store.wait()


def body(observed, block_mask, plan, cell_factors, region_factors):
    total_cols = lax.axis_size("region") * ROWS
    scale = 0.5 / math.sqrt(total_cols)
    rate = total_cols / ROWS
    dma = pltpu.SemaphoreType.DMA
    f32, bf16 = jnp.float32, jnp.bfloat16
    anywhere = pl.BlockSpec(memory_space=pl.ANY)
    out = jax.ShapeDtypeStruct((ROWS, RANK), f32)
    return pl.pallas_call(
        functools.partial(kernel, scale, rate),
        name="epoch",
        out_shape=(out, out),
        in_specs=[
            pl.BlockSpec(memory_space=pltpu.SMEM),
            pl.BlockSpec(memory_space=pltpu.VMEM),
            anywhere,
            anywhere,
            anywhere,
        ],
        out_specs=(anywhere, anywhere),
        scratch_shapes=[
            pltpu.VMEM((STRATA, ROWS, ROWS), bf16),
            pltpu.VMEM((10, ROWS, RANK), f32),
            pltpu.VMEM((STRATA + 1, ROWS, RANK), f32),
            pltpu.VMEM((STRATA, ROWS, RANK), f32),
            pltpu.VMEM((STRATA, HALF, RANK), f32),
            pltpu.VMEM((STRATA, 8, PIECE, RANK), f32),
            pltpu.VMEM((STRATA, ROWS // 8, ROWS), f32),
            pltpu.VMEM((ROWS, CHUNK), bf16),
            pltpu.VMEM((ROWS, RANK), bf16),
            pltpu.VMEM((ROWS, RANK), bf16),
            pltpu.VMEM((PIECE, RANK), f32),
            dma((2 + STRATA,)),
            dma((3, CHUNKS)),
            dma((7, CHUNKS)),
            dma((3, CHUNKS)),
            dma((STRATA,)),
            dma((STRATA,)),
            dma((STRATA, 8)),
            dma((STRATA, 8)),
            dma((STRATA, 8)),
            dma((STRATA, 8)),
            dma((STRATA, 8)),
            dma((STRATA, 8)),
            dma((RETS,)),
            dma((2, RETS)),
            dma((RETS,)),
            dma((RETS,)),
            dma((RETS,)),
            dma((RETS,)),
            dma((RETS + 1,)),
        ],
        compiler_params=pltpu.CompilerParams(
            collective_id=0, has_side_effects=True, vmem_limit_bytes=56 * 2**20
        ),
    )(plan, block_mask, observed, cell_factors, region_factors)


def solution(mesh):
    in_specs = (
        P("cell", "region"),
        P("cell", "region"),
        P(),
        P("cell", None),
        P(("cell", "region"), None),
    )
    out_specs = (P("cell", None), P(("cell", "region"), None))
    return jax.shard_map(body, mesh=mesh, in_specs=in_specs, out_specs=out_specs, check_vma=False)
```

```python
import functools
import math

import jax
import jax.numpy as jnp
from jax import lax
from jax.experimental import pallas as pl
from jax.experimental.pallas import tpu as pltpu
from jax.sharding import PartitionSpec as P

STRATA = 4
MOMENTUM = 0.9
ROWS = 1024
RANK = 256
CHUNK = 256
CHUNKS = ROWS // CHUNK
HALF = ROWS // 2
PIECE = 64
RET = 128
RETS = ROWS // RET
DOWN = (0, 2, 4)
RAW, FINAL, RELAY = 4, 7, 8
NT = (((1,), (1,)), ((), ()))
TN = (((0,), (0,)), ((), ()))


def remote(src, dst, send, recv, cell, region):
    return pltpu.make_async_remote_copy(
        src_ref=src,
        dst_ref=dst,
        send_sem=send,
        recv_sem=recv,
        device_id={"cell": cell, "region": region},
        device_id_type=pl.DeviceIdType.MESH,
    )


def kernel(
    scale, rate, plan, mask, y_hbm, u_hbm, v_hbm, out_u, out_v,
    ybuf, vbuf, ubuf, gbuf, core_buf, sum_buf, expanded, resid, u_bf, u_scaled, moment,
    load_sem, shift_send, shift_recv, pass_send,
    core_send, core_recv, rs_send, rs_recv, ag_send, ag_recv, agc_send, agc_recv,
    ret_send, ret_recv, relay_send, relay_recv,
):
    cell, region = lax.axis_index("cell"), lax.axis_index("region")
    z, core, chip = cell % 8, region % 2, region // 2
    ring = cell - z
    across = (cell + 8) % 16
    other_core = region + 1 - 2 * core

    def along(steps):
        return ring + (z + steps + 8) % 8

    x, y = chip // 2, chip % 2
    level = region + 2 - 4 * y

    def peer(d):
        return (region + 4 * d) % 16

    def v_rows(slot, k):
        return vbuf.at[slot, pl.ds(k * CHUNK, CHUNK)]

    def ret_rows(slot, p):
        return vbuf.at[slot, pl.ds(p * RET, RET)]

    loads = [
        pltpu.make_async_copy(u_hbm, ubuf.at[0], load_sem.at[0]),
        pltpu.make_async_copy(v_hbm, vbuf.at[0], load_sem.at[1]),
    ] + [
        pltpu.make_async_copy(y_hbm.at[:, pl.ds(q * ROWS, ROWS)], ybuf.at[q], load_sem.at[2 + q]) for q in range(STRATA)
    ]
    for load in loads:
        load.start()

    barrier = pltpu.get_barrier_semaphore()
    greeted = [(cell, other_core)] + [(cell, level)] + [(cell, peer(d)) for d in (1, 2, 3)]
    greeted += [(along(d), region) for d in (-1, 1, -3, 3)] + [(across, region)]
    last = (cell + 13) % 16
    sender = last - last % 8 + (last % 8 + 5) % 8
    greeted += [((cell + 3) % 16, region), ((along(3) + 3) % 16, region)]
    greeted += [(last, region), (sender, region)]
    for c, r in greeted:
        pl.semaphore_signal(
            barrier, inc=1, device_id={"cell": c, "region": r}, device_id_type=pl.DeviceIdType.MESH
        )
    moment[...] = jnp.zeros_like(moment)
    mask_bf = mask[...].astype(jnp.float32).astype(jnp.bfloat16)
    block = lax.broadcasted_iota(jnp.int32, (32, ROWS), 0)
    lane = lax.broadcasted_iota(jnp.int32, (32, ROWS), 1)
    for q in range(STRATA):
        chosen = (block == q * 8 + lane // 128).astype(jnp.float32).astype(jnp.bfloat16)
        expanded[q] = lax.dot_general(mask_bf, chosen, TN, preferred_element_type=jnp.float32)
    for load in loads:
        load.wait()
    pl.semaphore_wait(barrier, len(greeted))

    is0 = 1 - (z + 7) // 8
    mine = core * HALF + chip * PIECE

    def shift_copy(s, k):
        slot = s + 1 + is0 * (RAW - 1)
        first = along(-1)
        to = first if k < 2 else first + is0 * (across - first)
        return remote(v_rows(s, k), v_rows(slot, k), shift_send.at[s, k], shift_recv.at[slot, k], to, region)

    def shift_copy_in(s, k):
        remote(v_rows(s, k), v_rows(s, k), shift_send.at[0, k], shift_recv.at[s, k], cell, region).wait_recv()

    def pass_on(s, k, to):
        remote(v_rows(RAW + s, k), v_rows(RAW + s, k), pass_send.at[s, k], shift_recv.at[RAW + s, k], to, region).wait_recv()
        remote(v_rows(RAW + s, k), v_rows(s + 1, k), pass_send.at[s, k], shift_recv.at[s + 1, k], to, region).start()

    def pass_wait(s, k, to):
        remote(v_rows(RAW + s, k), v_rows(s + 1, k), pass_send.at[s, k], shift_recv.at[s + 1, k], to, region).wait_send()

    def ret_copy(p):
        return remote(ret_rows(3, p), ret_rows(FINAL, p), ret_send.at[p], ret_recv.at[p], (cell + 3) % 16, region)

    def ret_copy_down(p):
        return remote(ret_rows(3, p), ret_rows(RELAY, p), ret_send.at[p], relay_recv.at[p], along(-3), region)

    def relay_copy(p):
        home = (along(3) + 3) % 16
        return remote(ret_rows(RELAY, p), ret_rows(FINAL, p), relay_send.at[p], ret_recv.at[p], home, region)

    def ret_in(p):
        rows = ret_rows(FINAL, p)
        return remote(rows, rows, ret_send.at[p], ret_recv.at[p], cell, region)

    def core_copy(s):
        away = pl.ds((1 - core) * HALF, HALF)
        return remote(gbuf.at[s, away], core_buf.at[s], core_send.at[s], core_recv.at[s], cell, other_core)

    def piece(px, py):
        return pl.ds(core * HALF + ((px + 4) % 4 * 2 + py) * PIECE, PIECE)

    def rs_copy(s, far, d):
        i = 3 * far + d - 1
        rows = piece(x + d, y + far - 2 * far * y)
        return remote(gbuf.at[s, rows], sum_buf.at[s, i], rs_send.at[s, i], rs_recv.at[s, i], cell, peer(d))

    def rs_copy_y(s):
        rows = piece(x, 1 - y)
        return remote(gbuf.at[s, rows], sum_buf.at[s, 6], rs_send.at[s, 6], rs_recv.at[s, 6], cell, level)

    def ag_copy(s, i, px, py, to):
        rows = ubuf.at[s + 1, piece(px, py)]
        return remote(rows, rows, ag_send.at[s, i], ag_recv.at[s, i], cell, to)

    def ag_near(s, d):
        return ag_copy(s, d - 1, x, y, peer(d))

    def ag_far(s, d):
        return ag_copy(s, 2 + d, x, 1 - y, peer(d))

    def ag_y(s):
        return ag_copy(s, 6, x, y, level)

    def agc_copy(s, i, px, py):
        rows = ubuf.at[s + 1, piece(px, py)]
        return remote(rows, rows, agc_send.at[s, i], agc_recv.at[s, i], cell, other_core)

    def prepare(s):
        u = ubuf[s].astype(jnp.bfloat16)
        u_bf[...] = u
        u_scaled[...] = u * jnp.bfloat16(scale)

    def chunk(s, k):
        v_bf = vbuf[s, pl.ds(k * CHUNK, CHUNK), :].astype(jnp.bfloat16)
        q, columns = plan[s], pl.ds(k * CHUNK, CHUNK)
        for m in range(4):
            base = pl.multiple_of(((1 - core) * HALF + m * 256) % ROWS, 256)
            rows = pl.ds(base, 256)
            predicted = lax.dot_general(u_scaled[rows, :], v_bf, NT, preferred_element_type=jnp.float32)
            w = expanded[q, pl.ds(pl.multiple_of(base // 8, 32), 32), columns]
            w = jnp.broadcast_to(w[:, None, :], (32, 8, CHUNK)).reshape(256, CHUNK)
            r = (w * (predicted - ybuf[q, rows, columns].astype(jnp.float32))).astype(jnp.bfloat16)
            resid[rows, :] = r
            g = scale * jnp.dot(r, v_bf, preferred_element_type=jnp.float32)
            gbuf[s, rows, :] = g if k == 0 else gbuf[s, rows, :] + g
            if k == CHUNKS - 1 and m == 1:
                core_copy(s).start()
        h = scale * lax.dot_general(resid[...], u_bf[...], TN, preferred_element_type=jnp.float32)
        vbuf[s, pl.ds(k * CHUNK, CHUNK), :] = vbuf[s, pl.ds(k * CHUNK, CHUNK), :] - rate * h

    def reduce_core(s):
        core_copy(s).wait_recv()
        own = pl.ds(pl.multiple_of(core * HALF, HALF), HALF)
        gbuf[s, own, :] = gbuf[s, own, :] + core_buf[s]
        for far in (1, 0):
            for d in (2, 1, 3):
                rs_copy(s, far, d).start()

    def aligned(px, py):
        return pl.ds(pl.multiple_of(core * HALF + (px * 2 + py) * PIECE, PIECE), PIECE)

    def reduce_far(s):
        rows = aligned(x, 1 - y)
        total = gbuf[s, rows, :]
        for d in (1, 3, 2):
            rs_copy(s, 1, d).wait_recv()
            total = total + sum_buf[s, 2 + d]
        gbuf[s, rows, :] = total
        rs_copy_y(s).start()

    def reduce_near(s):
        rows = aligned(x, y)
        total = gbuf[s, rows, :]
        for d in (1, 3, 2):
            rs_copy(s, 0, d).wait_recv()
            total = total + sum_buf[s, d - 1]
        rs_copy_y(s).wait_recv()
        step = MOMENTUM * moment[...] + (total + sum_buf[s, 6])
        moment[...] = step
        ubuf[s + 1, rows, :] = ubuf[s, rows, :] - step
        ag_y(s).start()
        for d in (2, 1, 3):
            ag_near(s, d).start()
        agc_copy(s, 6, x, y).start()

    def gather_y(s):
        ag_y(s).wait_recv()
        for d in (2, 1, 3):
            ag_far(s, d).start()
        agc_copy(s, 7, x, 1 - y).start()

    def gather(s):
        for d in (1, 3, 2):
            ag_near(s, d).wait_recv()
            agc_copy(s, d - 1, x - d, y).start()
        for d in (1, 3, 2):
            ag_far(s, d).wait_recv()
            agc_copy(s, 2 + d, x - d, 1 - y).start()
        for i in range(8):
            agc_copy(s, i, x, y).wait_recv()

    @pl.loop(0, STRATA - 1)
    def _(s):
        prepare(s)
        for k in range(CHUNKS):
            @pl.when(s > 0)
            def _():
                shift_copy_in(s, k)
            chunk(s, k)
            shift_copy(s, k).start()
        reduce_core(s)
        reduce_far(s)

        @pl.when(z == 7)
        def _():
            pass_on(s, 0, across)

        @pl.when(z == 0)
        def _():
            pass_on(s, 2, along(-1))

        reduce_near(s)

        @pl.when(z == 7)
        def _():
            pass_on(s, 1, across)

        gather_y(s)

        @pl.when(z == 0)
        def _():
            pass_on(s, 3, along(-1))

        gather(s)

    s = STRATA - 1
    prepare(s)
    for k in range(CHUNKS):
        shift_copy_in(s, k)
        chunk(s, k)
        for p in (2 * k, 2 * k + 1):
            (ret_copy_down(p) if p in DOWN else ret_copy(p)).start()
    reduce_core(s)

    def relay(p):
        ret_copy_down(p).wait_recv()
        relay_copy(p).start()

    reduce_far(s)
    relay(DOWN[0])
    reduce_near(s)
    gather_y(s)
    relay(DOWN[1])
    gather(s)
    out_u[...] = ubuf[STRATA]
    relay(DOWN[2])

    order = (1, 3, 0, 5, 2, 6, 4, 7)

    for p in order:
        ret_in(p).wait_recv()
        out_v[pl.ds(p * RET, RET), :] = vbuf[FINAL, pl.ds(p * RET, RET), :]

    @pl.loop(0, STRATA)
    def _(s):
        core_copy(s).wait_send()
        rs_copy_y(s).wait_send()
        ag_y(s).wait_send()
        for d in (1, 2, 3):
            rs_copy(s, 0, d).wait_send()
            rs_copy(s, 1, d).wait_send()
            ag_near(s, d).wait_send()
            ag_far(s, d).wait_send()
        for i in range(8):
            agc_copy(s, i, x, y).wait_send()

    @pl.loop(0, STRATA - 1)
    def _(s):
        for k in range(CHUNKS):
            shift_copy(s, k).wait_send()

        @pl.when(z == 7)
        def _():
            pass_wait(s, 0, across)
            pass_wait(s, 1, across)

        @pl.when(z == 0)
        def _():
            pass_wait(s, 2, along(-1))
            pass_wait(s, 3, along(-1))

    for p in range(RETS):
        (ret_copy_down(p) if p in DOWN else ret_copy(p)).wait_send()
    for p in DOWN:
        relay_copy(p).wait_send()


def body(observed, block_mask, plan, cell_factors, region_factors):
    total_cols = lax.axis_size("region") * ROWS
    scale = 0.5 / math.sqrt(total_cols)
    rate = total_cols / ROWS
    dma = pltpu.SemaphoreType.DMA
    f32, bf16 = jnp.float32, jnp.bfloat16
    anywhere = pl.BlockSpec(memory_space=pl.ANY)
    out = pltpu.VMEM((ROWS, RANK), f32)
    return pl.pallas_call(
        functools.partial(kernel, scale, rate),
        name="epoch",
        out_shape=(out, out),
        in_specs=[
            pl.BlockSpec(memory_space=pltpu.SMEM),
            pl.BlockSpec(memory_space=pltpu.VMEM),
            anywhere,
            anywhere,
            anywhere,
        ],
        out_specs=(pl.BlockSpec(memory_space=pltpu.VMEM),) * 2,
        scratch_shapes=[
            pltpu.VMEM((STRATA, ROWS, ROWS), bf16),
            pltpu.VMEM((9, ROWS, RANK), f32),
            pltpu.VMEM((STRATA + 1, ROWS, RANK), f32),
            pltpu.VMEM((STRATA, ROWS, RANK), f32),
            pltpu.VMEM((STRATA, HALF, RANK), f32),
            pltpu.VMEM((STRATA, 8, PIECE, RANK), f32),
            pltpu.VMEM((STRATA, ROWS // 8, ROWS), f32),
            pltpu.VMEM((ROWS, CHUNK), bf16),
            pltpu.VMEM((ROWS, RANK), bf16),
            pltpu.VMEM((ROWS, RANK), bf16),
            pltpu.VMEM((PIECE, RANK), f32),
            dma((2 + STRATA,)),
            dma((3, CHUNKS)),
            dma((7, CHUNKS)),
            dma((3, CHUNKS)),
            dma((STRATA,)),
            dma((STRATA,)),
            dma((STRATA, 8)),
            dma((STRATA, 8)),
            dma((STRATA, 8)),
            dma((STRATA, 8)),
            dma((STRATA, 8)),
            dma((STRATA, 8)),
            dma((RETS,)),
            dma((RETS,)),
            dma((RETS,)),
            dma((RETS,)),
        ],
        compiler_params=pltpu.CompilerParams(
            collective_id=0, has_side_effects=True, vmem_limit_bytes=56 * 2**20
        ),
    )(plan, block_mask.T, observed, cell_factors, region_factors)


def solution(mesh):
    in_specs = (
        P("cell", "region"),
        P("cell", "region"),
        P(),
        P("cell", None),
        P(("cell", "region"), None),
    )
    out_specs = (P("cell", None), P(("cell", "region"), None))
    return jax.shard_map(body, mesh=mesh, in_specs=in_specs, out_specs=out_specs, check_vma=False)
```

```python
import functools
import math

import jax
import jax.numpy as jnp
from jax import lax
from jax.experimental import pallas as pl
from jax.experimental.pallas import tpu as pltpu
from jax.sharding import PartitionSpec as P

STRATA = 4
MOMENTUM = 0.9
ROWS = 1024
RANK = 256
CHUNK = 256
CHUNKS = ROWS // CHUNK
HALF = ROWS // 2
PIECE = 64
RET = 128
RETS = ROWS // RET
ROUTES = "PDPD"
DOWN = (0, 2, 4)
TURNS = (5, 7)
RAW, FINAL, RELAY, TURN = 4, 7, 8, 9
NT = (((1,), (1,)), ((), ()))
TN = (((0,), (0,)), ((), ()))


def remote(src, dst, send, recv, cell, region):
    return pltpu.make_async_remote_copy(
        src_ref=src,
        dst_ref=dst,
        send_sem=send,
        recv_sem=recv,
        device_id={"cell": cell, "region": region},
        device_id_type=pl.DeviceIdType.MESH,
    )


def kernel(
    scale, rate, plan, mask, y_hbm, u_hbm, v_hbm, out_u, out_v,
    ybuf, vbuf, ubuf, gbuf, core_buf, sum_buf, expanded, resid, u_bf, u_scaled, moment,
    load_sem, shift_send, shift_recv, pass_send,
    core_send, core_recv, rs_send, rs_recv, ag_send, ag_recv, agc_send, agc_recv,
    ret_send, ret_recv, relay_send, relay_recv, turn_send,
):
    cell, region = lax.axis_index("cell"), lax.axis_index("region")
    z, core, chip = cell % 8, region % 2, region // 2
    ring = cell - z
    across = (cell + 8) % 16
    other_core = region + 1 - 2 * core

    def along(steps):
        return ring + (z + steps + 8) % 8

    x, y = chip // 2, chip % 2
    level = region + 2 - 4 * y

    def peer(d):
        return (region + 4 * d) % 16

    def v_rows(slot, k):
        return vbuf.at[slot, pl.ds(k * CHUNK, CHUNK)]

    def ret_rows(slot, p):
        return vbuf.at[slot, pl.ds(p * RET, RET)]

    loads = [
        pltpu.make_async_copy(u_hbm, ubuf.at[0], load_sem.at[0]),
        pltpu.make_async_copy(v_hbm, vbuf.at[0], load_sem.at[1]),
    ] + [
        pltpu.make_async_copy(y_hbm.at[:, pl.ds(q * ROWS, ROWS)], ybuf.at[q], load_sem.at[2 + q]) for q in range(STRATA)
    ]
    for load in loads:
        load.start()

    barrier = pltpu.get_barrier_semaphore()
    greeted = [(cell, other_core)] + [(cell, level)] + [(cell, peer(d)) for d in (1, 2, 3)]
    greeted += [(along(d), region) for d in (-1, 1, -3, 3)] + [(across, region)]
    last = (cell + 13) % 16
    sender = last - last % 8 + (last % 8 + 5) % 8
    greeted += [((cell + 3) % 16, region), ((along(3) + 3) % 16, region)]
    greeted += [((cell + 15) % 16, region), ((cell + 1) % 16, region)]
    greeted += [(last, region), (sender, region)]
    for c, r in greeted:
        pl.semaphore_signal(
            barrier, inc=1, device_id={"cell": c, "region": r}, device_id_type=pl.DeviceIdType.MESH
        )
    moment[...] = jnp.zeros_like(moment)
    mask_bf = mask[...].astype(jnp.float32).astype(jnp.bfloat16)
    block = lax.broadcasted_iota(jnp.int32, (32, ROWS), 0)
    lane = lax.broadcasted_iota(jnp.int32, (32, ROWS), 1)
    for q in range(STRATA):
        chosen = (block == q * 8 + lane // 128).astype(jnp.float32).astype(jnp.bfloat16)
        expanded[q] = lax.dot_general(mask_bf, chosen, TN, preferred_element_type=jnp.float32)
    for load in loads:
        load.wait()
    pl.semaphore_wait(barrier, len(greeted))

    is0 = 1 - (z + 7) // 8
    mine = core * HALF + chip * PIECE

    def shift_copy(s, k):
        near = along(-1)
        next_cell = (cell + 15) % 16
        slot = s + 1 if ROUTES[k] == "D" else s + 1 + is0 * (RAW - 1)
        to = {"D": next_cell, "Q": near, "P": near + is0 * (across - near)}[ROUTES[k]]
        return remote(v_rows(s, k), v_rows(slot, k), shift_send.at[s, k], shift_recv.at[slot, k], to, region)

    def shift_copy_in(s, k):
        remote(v_rows(s, k), v_rows(s, k), shift_send.at[0, k], shift_recv.at[s, k], cell, region).wait_recv()

    def pass_on(s, k, to):
        remote(v_rows(RAW + s, k), v_rows(RAW + s, k), pass_send.at[s, k], shift_recv.at[RAW + s, k], to, region).wait_recv()
        remote(v_rows(RAW + s, k), v_rows(s + 1, k), pass_send.at[s, k], shift_recv.at[s + 1, k], to, region).start()

    def pass_wait(s, k, to):
        remote(v_rows(RAW + s, k), v_rows(s + 1, k), pass_send.at[s, k], shift_recv.at[s + 1, k], to, region).wait_send()

    def ret_copy(p):
        home = (cell + 3) % 16
        turns = (z + 3) // 8 if p in TURNS else 0
        slot, to = FINAL + turns * (TURN - FINAL), home + turns * (across - home)
        return remote(ret_rows(3, p), ret_rows(slot, p), ret_send.at[p], ret_recv.at[turns, p], to, region)

    def turn_in(p):
        rows = ret_rows(TURN, p)
        return remote(rows, rows, ret_send.at[p], ret_recv.at[1, p], cell, region)

    def turn_copy(p):
        return remote(ret_rows(TURN, p), ret_rows(FINAL, p), turn_send.at[p], ret_recv.at[0, p], along(3), region)

    def ret_copy_down(p):
        return remote(ret_rows(3, p), ret_rows(RELAY, p), ret_send.at[p], relay_recv.at[p], along(-3), region)

    def relay_copy(p):
        home = (along(3) + 3) % 16
        return remote(ret_rows(RELAY, p), ret_rows(FINAL, p), relay_send.at[p], ret_recv.at[0, p], home, region)

    def ret_in(p):
        rows = ret_rows(FINAL, p)
        return remote(rows, rows, ret_send.at[p], ret_recv.at[0, p], cell, region)

    def core_copy(s):
        away = pl.ds((1 - core) * HALF, HALF)
        return remote(gbuf.at[s, away], core_buf.at[s], core_send.at[s], core_recv.at[s], cell, other_core)

    def piece(px, py):
        return pl.ds(core * HALF + ((px + 4) % 4 * 2 + py) * PIECE, PIECE)

    def rs_copy(s, far, d):
        i = 3 * far + d - 1
        rows = piece(x + d, y + far - 2 * far * y)
        return remote(gbuf.at[s, rows], sum_buf.at[s, i], rs_send.at[s, i], rs_recv.at[s, i], cell, peer(d))

    def rs_copy_y(s):
        rows = piece(x, 1 - y)
        return remote(gbuf.at[s, rows], sum_buf.at[s, 6], rs_send.at[s, 6], rs_recv.at[s, 6], cell, level)

    def ag_copy(s, i, px, py, to):
        rows = ubuf.at[s + 1, piece(px, py)]
        return remote(rows, rows, ag_send.at[s, i], ag_recv.at[s, i], cell, to)

    def ag_near(s, d):
        return ag_copy(s, d - 1, x, y, peer(d))

    def ag_far(s, d):
        return ag_copy(s, 2 + d, x, 1 - y, peer(d))

    def ag_y(s):
        return ag_copy(s, 6, x, y, level)

    def agc_copy(s, i, px, py):
        rows = ubuf.at[s + 1, piece(px, py)]
        return remote(rows, rows, agc_send.at[s, i], agc_recv.at[s, i], cell, other_core)

    def prepare(s):
        u = ubuf[s].astype(jnp.bfloat16)
        u_bf[...] = u
        u_scaled[...] = u * jnp.bfloat16(scale)

    def chunk(s, k):
        v_bf = vbuf[s, pl.ds(k * CHUNK, CHUNK), :].astype(jnp.bfloat16)
        q, columns = plan[s], pl.ds(k * CHUNK, CHUNK)
        for m in range(4):
            base = pl.multiple_of(((1 - core) * HALF + m * 256) % ROWS, 256)
            rows = pl.ds(base, 256)
            predicted = lax.dot_general(u_scaled[rows, :], v_bf, NT, preferred_element_type=jnp.float32)
            w = expanded[q, pl.ds(pl.multiple_of(base // 8, 32), 32), columns]
            w = jnp.broadcast_to(w[:, None, :], (32, 8, CHUNK)).reshape(256, CHUNK)
            r = (w * (predicted - ybuf[q, rows, columns].astype(jnp.float32))).astype(jnp.bfloat16)
            resid[rows, :] = r
            g = scale * jnp.dot(r, v_bf, preferred_element_type=jnp.float32)
            gbuf[s, rows, :] = g if k == 0 else gbuf[s, rows, :] + g
            if k == CHUNKS - 1 and m == 1:
                core_copy(s).start()
        h = scale * lax.dot_general(resid[...], u_bf[...], TN, preferred_element_type=jnp.float32)
        vbuf[s, pl.ds(k * CHUNK, CHUNK), :] = vbuf[s, pl.ds(k * CHUNK, CHUNK), :] - rate * h

    def reduce_core(s):
        core_copy(s).wait_recv()
        own = pl.ds(pl.multiple_of(core * HALF, HALF), HALF)
        gbuf[s, own, :] = gbuf[s, own, :] + core_buf[s]
        for far in (1, 0):
            for d in (2, 1, 3):
                rs_copy(s, far, d).start()

    def aligned(px, py):
        return pl.ds(pl.multiple_of(core * HALF + (px * 2 + py) * PIECE, PIECE), PIECE)

    def reduce_far(s):
        rows = aligned(x, 1 - y)
        total = gbuf[s, rows, :]
        for d in (1, 3, 2):
            rs_copy(s, 1, d).wait_recv()
            total = total + sum_buf[s, 2 + d]
        gbuf[s, rows, :] = total
        rs_copy_y(s).start()

    def reduce_near(s):
        rows = aligned(x, y)
        total = gbuf[s, rows, :]
        for d in (1, 3, 2):
            rs_copy(s, 0, d).wait_recv()
            total = total + sum_buf[s, d - 1]
        rs_copy_y(s).wait_recv()
        step = MOMENTUM * moment[...] + (total + sum_buf[s, 6])
        moment[...] = step
        ubuf[s + 1, rows, :] = ubuf[s, rows, :] - step
        ag_y(s).start()
        for d in (2, 1, 3):
            ag_near(s, d).start()
        agc_copy(s, 6, x, y).start()

    def gather_y(s):
        ag_y(s).wait_recv()
        for d in (2, 1, 3):
            ag_far(s, d).start()
        agc_copy(s, 7, x, 1 - y).start()

    def gather(s):
        for d in (1, 3, 2):
            ag_near(s, d).wait_recv()
            agc_copy(s, d - 1, x - d, y).start()
        for d in (1, 3, 2):
            ag_far(s, d).wait_recv()
            agc_copy(s, 2 + d, x - d, 1 - y).start()
        for i in range(8):
            agc_copy(s, i, x, y).wait_recv()

    @pl.loop(0, STRATA - 1)
    def _(s):
        prepare(s)
        for k in range(CHUNKS):
            @pl.when(s > 0)
            def _():
                shift_copy_in(s, k)
            chunk(s, k)
            shift_copy(s, k).start()
        reduce_core(s)
        reduce_far(s)

        @pl.when(z == 0)
        def _():
            pass_on(s, 0, along(-1))

        reduce_near(s)

        gather_y(s)

        @pl.when(z == 0)
        def _():
            pass_on(s, 2, along(-1))

        gather(s)

    s = STRATA - 1
    prepare(s)
    for k in range(CHUNKS):
        shift_copy_in(s, k)
        chunk(s, k)
        for p in (2 * k, 2 * k + 1):
            (ret_copy_down(p) if p in DOWN else ret_copy(p)).start()
    reduce_core(s)

    @pl.when(z >= 5)
    def _():
        for p in TURNS:
            turn_in(p).wait_recv()
            turn_copy(p).start()

    def relay(p):
        ret_copy_down(p).wait_recv()
        relay_copy(p).start()

    reduce_far(s)
    relay(DOWN[0])
    reduce_near(s)
    gather_y(s)
    relay(DOWN[1])
    gather(s)
    out_u[...] = ubuf[STRATA]
    relay(DOWN[2])

    order = (1, 3, 0, 5, 2, 6, 4, 7)

    for p in order:
        ret_in(p).wait_recv()
        out_v[pl.ds(p * RET, RET), :] = vbuf[FINAL, pl.ds(p * RET, RET), :]

    @pl.loop(0, STRATA)
    def _(s):
        core_copy(s).wait_send()
        rs_copy_y(s).wait_send()
        ag_y(s).wait_send()
        for d in (1, 2, 3):
            rs_copy(s, 0, d).wait_send()
            rs_copy(s, 1, d).wait_send()
            ag_near(s, d).wait_send()
            ag_far(s, d).wait_send()
        for i in range(8):
            agc_copy(s, i, x, y).wait_send()

    @pl.loop(0, STRATA - 1)
    def _(s):
        for k in range(CHUNKS):
            shift_copy(s, k).wait_send()

        @pl.when(z == 0)
        def _():
            pass_wait(s, 0, along(-1))
            pass_wait(s, 2, along(-1))

    for p in range(RETS):
        (ret_copy_down(p) if p in DOWN else ret_copy(p)).wait_send()
    for p in DOWN:
        relay_copy(p).wait_send()

    @pl.when(z >= 5)
    def _():
        for p in TURNS:
            turn_copy(p).wait_send()


def body(observed, block_mask, plan, cell_factors, region_factors):
    total_cols = lax.axis_size("region") * ROWS
    scale = 0.5 / math.sqrt(total_cols)
    rate = total_cols / ROWS
    dma = pltpu.SemaphoreType.DMA
    f32, bf16 = jnp.float32, jnp.bfloat16
    anywhere = pl.BlockSpec(memory_space=pl.ANY)
    out = pltpu.VMEM((ROWS, RANK), f32)
    return pl.pallas_call(
        functools.partial(kernel, scale, rate),
        name="epoch",
        out_shape=(out, out),
        in_specs=[
            pl.BlockSpec(memory_space=pltpu.SMEM),
            pl.BlockSpec(memory_space=pltpu.VMEM),
            anywhere,
            anywhere,
            anywhere,
        ],
        out_specs=(pl.BlockSpec(memory_space=pltpu.VMEM),) * 2,
        scratch_shapes=[
            pltpu.VMEM((STRATA, ROWS, ROWS), bf16),
            pltpu.VMEM((10, ROWS, RANK), f32),
            pltpu.VMEM((STRATA + 1, ROWS, RANK), f32),
            pltpu.VMEM((STRATA, ROWS, RANK), f32),
            pltpu.VMEM((STRATA, HALF, RANK), f32),
            pltpu.VMEM((STRATA, 8, PIECE, RANK), f32),
            pltpu.VMEM((STRATA, ROWS // 8, ROWS), f32),
            pltpu.VMEM((ROWS, CHUNK), bf16),
            pltpu.VMEM((ROWS, RANK), bf16),
            pltpu.VMEM((ROWS, RANK), bf16),
            pltpu.VMEM((PIECE, RANK), f32),
            dma((2 + STRATA,)),
            dma((3, CHUNKS)),
            dma((7, CHUNKS)),
            dma((3, CHUNKS)),
            dma((STRATA,)),
            dma((STRATA,)),
            dma((STRATA, 8)),
            dma((STRATA, 8)),
            dma((STRATA, 8)),
            dma((STRATA, 8)),
            dma((STRATA, 8)),
            dma((STRATA, 8)),
            dma((RETS,)),
            dma((2, RETS)),
            dma((RETS,)),
            dma((RETS,)),
            dma((RETS,)),
        ],
        compiler_params=pltpu.CompilerParams(
            collective_id=0, has_side_effects=True, vmem_limit_bytes=56 * 2**20
        ),
    )(plan, block_mask.T, observed, cell_factors, region_factors)


def solution(mesh):
    in_specs = (
        P("cell", "region"),
        P("cell", "region"),
        P(),
        P("cell", None),
        P(("cell", "region"), None),
    )
    out_specs = (P("cell", None), P(("cell", "region"), None))
    return jax.shard_map(body, mesh=mesh, in_specs=in_specs, out_specs=out_specs, check_vma=False)
```

```python
import functools
import math

import jax
import jax.numpy as jnp
from jax import lax
from jax.experimental import pallas as pl
from jax.experimental.pallas import tpu as pltpu
from jax.sharding import PartitionSpec as P

STRATA = 4
MOMENTUM = 0.9
ROWS = 1024
RANK = 256
CHUNK = 256
CHUNKS = ROWS // CHUNK
HALF = ROWS // 2
PIECE = 64
RET = 128
RETS = ROWS // RET
ROUTES = "PDPD"
DOWN = (0, 2, 4)
TURNS = (5, 7)
RAW, FINAL, RELAY, TURN = 4, 7, 8, 9
NT = (((1,), (1,)), ((), ()))
TN = (((0,), (0,)), ((), ()))


def remote(src, dst, send, recv, cell, region):
    return pltpu.make_async_remote_copy(
        src_ref=src,
        dst_ref=dst,
        send_sem=send,
        recv_sem=recv,
        device_id={"cell": cell, "region": region},
        device_id_type=pl.DeviceIdType.MESH,
    )


def kernel(
    scale, rate, plan, mask, y_hbm, u_hbm, v_hbm, out_u, out_v,
    ybuf, vbuf, ubuf, gbuf, core_buf, sum_buf, expanded, resid, u_bf, u_scaled, moment,
    load_sem, shift_send, shift_recv, pass_send,
    core_send, core_recv, rs_send, rs_recv, ag_send, ag_recv, agc_send, agc_recv,
    ret_send, ret_recv, relay_send, relay_recv, turn_send,
):
    cell, region = lax.axis_index("cell"), lax.axis_index("region")
    z, core, chip = cell % 8, region % 2, region // 2
    ring = cell - z
    across = (cell + 8) % 16
    other_core = region + 1 - 2 * core

    def along(steps):
        return ring + (z + steps + 8) % 8

    x, y = chip // 2, chip % 2
    level = region + 2 - 4 * y

    def peer(d):
        return (region + 4 * d) % 16

    def v_rows(slot, k):
        return vbuf.at[slot, pl.ds(k * CHUNK, CHUNK)]

    def ret_rows(slot, p):
        return vbuf.at[slot, pl.ds(p * RET, RET)]

    loads = [
        pltpu.make_async_copy(u_hbm, ubuf.at[0], load_sem.at[0]),
        pltpu.make_async_copy(v_hbm, vbuf.at[0], load_sem.at[1]),
    ] + [
        pltpu.make_async_copy(y_hbm.at[:, pl.ds(q * ROWS, ROWS)], ybuf.at[q], load_sem.at[2 + q]) for q in range(STRATA)
    ]
    for load in loads:
        load.start()

    barrier = pltpu.get_barrier_semaphore()
    greeted = [(cell, other_core)] + [(cell, level)] + [(cell, peer(d)) for d in (1, 2, 3)]
    greeted += [(along(d), region) for d in (-1, 1, -3, 3)] + [(across, region)]
    last = (cell + 13) % 16
    sender = last - last % 8 + (last % 8 + 5) % 8
    greeted += [((cell + 3) % 16, region), ((along(3) + 3) % 16, region)]
    greeted += [((cell + 15) % 16, region), ((cell + 1) % 16, region)]
    greeted += [(last, region), (sender, region)]
    for c, r in greeted:
        pl.semaphore_signal(
            barrier, inc=1, device_id={"cell": c, "region": r}, device_id_type=pl.DeviceIdType.MESH
        )
    moment[...] = jnp.zeros_like(moment)
    mask_bf = mask[...].astype(jnp.float32).astype(jnp.bfloat16)
    block = lax.broadcasted_iota(jnp.int32, (32, ROWS), 0)
    lane = lax.broadcasted_iota(jnp.int32, (32, ROWS), 1)
    for q in range(STRATA):
        chosen = (block == q * 8 + lane // 128).astype(jnp.float32).astype(jnp.bfloat16)
        expanded[q] = lax.dot_general(mask_bf, chosen, TN, preferred_element_type=jnp.float32)
    for load in loads:
        load.wait()

    is0 = 1 - (z + 7) // 8
    mine = core * HALF + chip * PIECE

    def shift_copy(s, k):
        near = along(-1)
        next_cell = (cell + 15) % 16
        slot = s + 1 if ROUTES[k] == "D" else s + 1 + is0 * (RAW - 1)
        to = {"D": next_cell, "Q": near, "P": near + is0 * (across - near)}[ROUTES[k]]
        return remote(v_rows(s, k), v_rows(slot, k), shift_send.at[s, k], shift_recv.at[slot, k], to, region)

    def shift_copy_in(s, k):
        remote(v_rows(s, k), v_rows(s, k), shift_send.at[0, k], shift_recv.at[s, k], cell, region).wait_recv()

    def pass_on(s, k, to):
        remote(v_rows(RAW + s, k), v_rows(RAW + s, k), pass_send.at[s, k], shift_recv.at[RAW + s, k], to, region).wait_recv()
        remote(v_rows(RAW + s, k), v_rows(s + 1, k), pass_send.at[s, k], shift_recv.at[s + 1, k], to, region).start()

    def pass_wait(s, k, to):
        remote(v_rows(RAW + s, k), v_rows(s + 1, k), pass_send.at[s, k], shift_recv.at[s + 1, k], to, region).wait_send()

    def ret_copy(p):
        home = (cell + 3) % 16
        turns = (z + 3) // 8 if p in TURNS else 0
        slot, to = FINAL + turns * (TURN - FINAL), home + turns * (across - home)
        return remote(ret_rows(3, p), ret_rows(slot, p), ret_send.at[p], ret_recv.at[turns, p], to, region)

    def turn_in(p):
        rows = ret_rows(TURN, p)
        return remote(rows, rows, ret_send.at[p], ret_recv.at[1, p], cell, region)

    def turn_copy(p):
        return remote(ret_rows(TURN, p), ret_rows(FINAL, p), turn_send.at[p], ret_recv.at[0, p], along(3), region)

    def ret_copy_down(p):
        return remote(ret_rows(3, p), ret_rows(RELAY, p), ret_send.at[p], relay_recv.at[p], along(-3), region)

    def relay_copy(p):
        home = (along(3) + 3) % 16
        return remote(ret_rows(RELAY, p), ret_rows(FINAL, p), relay_send.at[p], ret_recv.at[0, p], home, region)

    def ret_in(p):
        rows = ret_rows(FINAL, p)
        return remote(rows, rows, ret_send.at[p], ret_recv.at[0, p], cell, region)

    def core_copy(s):
        away = pl.ds((1 - core) * HALF, HALF)
        return remote(gbuf.at[s, away], core_buf.at[s], core_send.at[s], core_recv.at[s], cell, other_core)

    def piece(px, py):
        return pl.ds(core * HALF + ((px + 4) % 4 * 2 + py) * PIECE, PIECE)

    def rs_copy(s, far, d):
        i = 3 * far + d - 1
        rows = piece(x + d, y + far - 2 * far * y)
        return remote(gbuf.at[s, rows], sum_buf.at[s, i], rs_send.at[s, i], rs_recv.at[s, i], cell, peer(d))

    def rs_copy_y(s):
        rows = piece(x, 1 - y)
        return remote(gbuf.at[s, rows], sum_buf.at[s, 6], rs_send.at[s, 6], rs_recv.at[s, 6], cell, level)

    def ag_copy(s, i, px, py, to):
        rows = ubuf.at[s + 1, piece(px, py)]
        return remote(rows, rows, ag_send.at[s, i], ag_recv.at[s, i], cell, to)

    def ag_near(s, d):
        return ag_copy(s, d - 1, x, y, peer(d))

    def ag_far(s, d):
        return ag_copy(s, 2 + d, x, 1 - y, peer(d))

    def ag_y(s):
        return ag_copy(s, 6, x, y, level)

    def agc_copy(s, i, px, py):
        rows = ubuf.at[s + 1, piece(px, py)]
        return remote(rows, rows, agc_send.at[s, i], agc_recv.at[s, i], cell, other_core)

    def prepare(s):
        u = ubuf[s].astype(jnp.bfloat16)
        u_bf[...] = u
        u_scaled[...] = u * jnp.bfloat16(scale)

    def chunk(s, k):
        v_bf = vbuf[s, pl.ds(k * CHUNK, CHUNK), :].astype(jnp.bfloat16)
        q, columns = plan[s], pl.ds(k * CHUNK, CHUNK)
        for m in range(4):
            base = pl.multiple_of(((1 - core) * HALF + m * 256) % ROWS, 256)
            rows = pl.ds(base, 256)
            predicted = lax.dot_general(u_scaled[rows, :], v_bf, NT, preferred_element_type=jnp.float32)
            w = expanded[q, pl.ds(pl.multiple_of(base // 8, 32), 32), columns]
            w = jnp.broadcast_to(w[:, None, :], (32, 8, CHUNK)).reshape(256, CHUNK)
            r = (w * (predicted - ybuf[q, rows, columns].astype(jnp.float32))).astype(jnp.bfloat16)
            resid[rows, :] = r
            g = scale * jnp.dot(r, v_bf, preferred_element_type=jnp.float32)
            gbuf[s, rows, :] = g if k == 0 else gbuf[s, rows, :] + g
            if k == CHUNKS - 1 and m == 1:
                core_copy(s).start()
        h = scale * lax.dot_general(resid[...], u_bf[...], TN, preferred_element_type=jnp.float32)
        vbuf[s, pl.ds(k * CHUNK, CHUNK), :] = vbuf[s, pl.ds(k * CHUNK, CHUNK), :] - rate * h

    def reduce_core(s):
        core_copy(s).wait_recv()
        own = pl.ds(pl.multiple_of(core * HALF, HALF), HALF)
        gbuf[s, own, :] = gbuf[s, own, :] + core_buf[s]
        for far in (1, 0):
            for d in (2, 1, 3):
                rs_copy(s, far, d).start()

    def aligned(px, py):
        return pl.ds(pl.multiple_of(core * HALF + (px * 2 + py) * PIECE, PIECE), PIECE)

    def reduce_far(s):
        rows = aligned(x, 1 - y)
        total = gbuf[s, rows, :]
        for d in (1, 3, 2):
            rs_copy(s, 1, d).wait_recv()
            total = total + sum_buf[s, 2 + d]
        gbuf[s, rows, :] = total
        rs_copy_y(s).start()

    def reduce_near(s):
        rows = aligned(x, y)
        total = gbuf[s, rows, :]
        for d in (1, 3, 2):
            rs_copy(s, 0, d).wait_recv()
            total = total + sum_buf[s, d - 1]
        rs_copy_y(s).wait_recv()
        step = MOMENTUM * moment[...] + (total + sum_buf[s, 6])
        moment[...] = step
        ubuf[s + 1, rows, :] = ubuf[s, rows, :] - step
        ag_y(s).start()
        for d in (2, 1, 3):
            ag_near(s, d).start()
        agc_copy(s, 6, x, y).start()

    def gather_y(s):
        ag_y(s).wait_recv()
        for d in (2, 1, 3):
            ag_far(s, d).start()
        agc_copy(s, 7, x, 1 - y).start()

    def gather(s):
        for d in (1, 3, 2):
            ag_near(s, d).wait_recv()
            agc_copy(s, d - 1, x - d, y).start()
        for d in (1, 3, 2):
            ag_far(s, d).wait_recv()
            agc_copy(s, 2 + d, x - d, 1 - y).start()
        for i in range(8):
            agc_copy(s, i, x, y).wait_recv()

    @pl.loop(0, STRATA - 1)
    def _(s):
        prepare(s)
        for k in range(CHUNKS):
            @pl.when(s > 0)
            def _():
                shift_copy_in(s, k)
            chunk(s, k)
            if k == 0:
                @pl.when(s == 0)
                def _():
                    pl.semaphore_wait(barrier, len(greeted))

            shift_copy(s, k).start()
        reduce_core(s)
        reduce_far(s)

        @pl.when(z == 0)
        def _():
            pass_on(s, 0, along(-1))

        reduce_near(s)

        gather_y(s)

        @pl.when(z == 0)
        def _():
            pass_on(s, 2, along(-1))

        gather(s)

    s = STRATA - 1
    prepare(s)
    for k in range(CHUNKS):
        shift_copy_in(s, k)
        chunk(s, k)
        for p in (2 * k, 2 * k + 1):
            (ret_copy_down(p) if p in DOWN else ret_copy(p)).start()
    reduce_core(s)

    @pl.when(z >= 5)
    def _():
        for p in TURNS:
            turn_in(p).wait_recv()
            turn_copy(p).start()

    def relay(p):
        ret_copy_down(p).wait_recv()
        relay_copy(p).start()

    reduce_far(s)
    relay(DOWN[0])
    reduce_near(s)
    gather_y(s)
    relay(DOWN[1])
    gather(s)
    out_u[...] = ubuf[STRATA]
    relay(DOWN[2])

    order = (1, 3, 0, 5, 2, 6, 4, 7)

    for p in order:
        ret_in(p).wait_recv()
        out_v[pl.ds(p * RET, RET), :] = vbuf[FINAL, pl.ds(p * RET, RET), :]

    @pl.loop(0, STRATA)
    def _(s):
        core_copy(s).wait_send()
        rs_copy_y(s).wait_send()
        ag_y(s).wait_send()
        for d in (1, 2, 3):
            rs_copy(s, 0, d).wait_send()
            rs_copy(s, 1, d).wait_send()
            ag_near(s, d).wait_send()
            ag_far(s, d).wait_send()
        for i in range(8):
            agc_copy(s, i, x, y).wait_send()

    @pl.loop(0, STRATA - 1)
    def _(s):
        for k in range(CHUNKS):
            shift_copy(s, k).wait_send()

        @pl.when(z == 0)
        def _():
            pass_wait(s, 0, along(-1))
            pass_wait(s, 2, along(-1))

    for p in range(RETS):
        (ret_copy_down(p) if p in DOWN else ret_copy(p)).wait_send()
    for p in DOWN:
        relay_copy(p).wait_send()

    @pl.when(z >= 5)
    def _():
        for p in TURNS:
            turn_copy(p).wait_send()


def body(observed, block_mask, plan, cell_factors, region_factors):
    total_cols = lax.axis_size("region") * ROWS
    scale = 0.5 / math.sqrt(total_cols)
    rate = total_cols / ROWS
    dma = pltpu.SemaphoreType.DMA
    f32, bf16 = jnp.float32, jnp.bfloat16
    anywhere = pl.BlockSpec(memory_space=pl.ANY)
    out = pltpu.VMEM((ROWS, RANK), f32)
    return pl.pallas_call(
        functools.partial(kernel, scale, rate),
        name="epoch",
        out_shape=(out, out),
        in_specs=[
            pl.BlockSpec(memory_space=pltpu.SMEM),
            pl.BlockSpec(memory_space=pltpu.VMEM),
            anywhere,
            anywhere,
            anywhere,
        ],
        out_specs=(pl.BlockSpec(memory_space=pltpu.VMEM),) * 2,
        scratch_shapes=[
            pltpu.VMEM((STRATA, ROWS, ROWS), bf16),
            pltpu.VMEM((10, ROWS, RANK), f32),
            pltpu.VMEM((STRATA + 1, ROWS, RANK), f32),
            pltpu.VMEM((STRATA, ROWS, RANK), f32),
            pltpu.VMEM((STRATA, HALF, RANK), f32),
            pltpu.VMEM((STRATA, 8, PIECE, RANK), f32),
            pltpu.VMEM((STRATA, ROWS // 8, ROWS), f32),
            pltpu.VMEM((ROWS, CHUNK), bf16),
            pltpu.VMEM((ROWS, RANK), bf16),
            pltpu.VMEM((ROWS, RANK), bf16),
            pltpu.VMEM((PIECE, RANK), f32),
            dma((2 + STRATA,)),
            dma((3, CHUNKS)),
            dma((7, CHUNKS)),
            dma((3, CHUNKS)),
            dma((STRATA,)),
            dma((STRATA,)),
            dma((STRATA, 8)),
            dma((STRATA, 8)),
            dma((STRATA, 8)),
            dma((STRATA, 8)),
            dma((STRATA, 8)),
            dma((STRATA, 8)),
            dma((RETS,)),
            dma((2, RETS)),
            dma((RETS,)),
            dma((RETS,)),
            dma((RETS,)),
        ],
        compiler_params=pltpu.CompilerParams(
            collective_id=0, has_side_effects=True, vmem_limit_bytes=56 * 2**20
        ),
    )(plan, block_mask.T, observed, cell_factors, region_factors)


def solution(mesh):
    in_specs = (
        P("cell", "region"),
        P("cell", "region"),
        P(),
        P("cell", None),
        P(("cell", "region"), None),
    )
    out_specs = (P("cell", None), P(("cell", "region"), None))
    return jax.shard_map(body, mesh=mesh, in_specs=in_specs, out_specs=out_specs, check_vma=False)
```
